128 devices in a mesh: seq: 8 (over z, core), exp: 16 (over y, x).
Axes of the slice: x: 4, y: 4, z: 4, core: 2. Of those that a mesh axis runs over, the one named last changes fastest.
Arguments:
- inputs: bfloat16 [16, 1024, 4096], P('exp', 'seq'), may hold values from -6 to 6
- b_proj: bfloat16 [16, 1024, 128], P('exp', 'seq'), may hold values from -0.046875 to 0.046875
- c_proj: bfloat16 [16, 1024, 128], P('exp', 'seq'), may hold values from -6 to 6
- log_decay: float32 [16, 32, 1024], P('exp', None, 'seq'), may hold values from -1.1 to 0, as said below
- doc_lengths: int32 [16, 6], P('exp'), may hold values from 1 to 512, 1024 in all within a row
- expert_ids: int32 [16, 1024, 2], P('exp', 'seq'), may hold values from 0 to 15, all different within a row; in each aligned block of 128 rows (0 to 127, 128 to 255, ..., all dimensions but the last counted through in order) at most 24 rows name the same one
- gate_weights: float32 [16, 1024, 2], P('exp', 'seq'), may hold values from 0.2 to 1
- w_up: bfloat16 [16, 4096, 1024], P('exp'), may hold values from -0.09375 to 0.09375
- w_down: bfloat16 [16, 1024, 4096], P('exp'), may hold values from -0.1875 to 0.1875
- cotangent: bfloat16 [16, 1024, 4096], P('exp', 'seq'), may hold values from -6 to 6
Outputs:
- output: bfloat16 [16, 1024, 4096], P('exp', 'seq')
- input_grad: bfloat16 [16, 1024, 4096], P('exp', 'seq')
The draws below stay inside these ranges and needn't reach their ends.
Inputs may be any that keep to these rules, and one draw needn't show every extreme that they name: `log_decay`: log of a decay factor, below zero. `doc_lengths`: each sequence's document lengths sum to 1024. `expert_ids`: two different experts a position; among the 128 positions of one device no expert is named more than 24 times, a bound that some block reaches.
All inputs are finite; a program needn't handle non-finite values.
Results may differ from the reference program's by a relative error of at most 0.013.
Values may be sent and summed in bfloat16 or wider, within the bound.
A program may use at most 128 MiB of HBM per device.

```python
import math
import jax
import jax.numpy as jnp
import numpy as np
from jax import lax

D = 4096
H = 32
P_SIZE = 128
N = 128
HID = 1024
BLOCK = 128
DOCS = 6
TOK_DEV = 128
STREAM_TOTAL = 16
STREAM_SPAN = 1024
EXPERTS = 16
CAP = 24
N_SEQ = 8
N_EXP = 16


def draw_log_decay(key, part):
    stochastic_seed_array = jax.random.split(key, 7)
    fast_share = 0.5
    head_pick = jax.random.uniform(stochastic_seed_array[0], (STREAM_TOTAL, H, 1))
    fast_rate = jnp.exp(jax.random.uniform(stochastic_seed_array[1], (STREAM_TOTAL, H, 1), minval=math.log(0.046), maxval=math.log(0.077)))
    slow_rate = jnp.exp(jax.random.uniform(stochastic_seed_array[2], (STREAM_TOTAL, H, 1), minval=math.log(0.05), maxval=math.log(0.4))) / STREAM_SPAN
    resting_frequency = jnp.where(head_pick < fast_share, fast_rate, slow_rate)
    each_chip_multiplier = jnp.exp(jax.random.uniform(stochastic_seed_array[3], (STREAM_TOTAL, H, STREAM_SPAN // TOK_DEV), minval=-0.693, maxval=0.693))
    each_chip_multiplier = jnp.repeat(each_chip_multiplier, TOK_DEV, axis=2)
    storage_unit_multiplier = jnp.exp(jax.random.uniform(stochastic_seed_array[4], (STREAM_TOTAL, H, STREAM_SPAN), minval=-0.693, maxval=0.693))
    spike_location = jax.random.randint(stochastic_seed_array[5], (STREAM_TOTAL, 2, 1), 0, STREAM_SPAN)
    spike_amplitude = jax.random.uniform(stochastic_seed_array[6], (STREAM_TOTAL, 2, 1), minval=math.log(0.5), maxval=math.log(0.8))
    element_offsets = jnp.arange(STREAM_SPAN, dtype=jnp.int32)[None, None, :]
    spike_attenuation = jnp.sum(jnp.where(spike_location == element_offsets, spike_amplitude, 0.0), axis=1)
    return (spike_attenuation[:, None, :] - resting_frequency * each_chip_multiplier * storage_unit_multiplier).astype(jnp.float32)


def steps_of(own_key, dims, pieces, smallest, high):
    def one(dim, shards_of):
        steps = jax.random.uniform(jax.random.fold_in(jax.random.fold_in(own_key, 6), dim), (shards_of,), jnp.float32, smallest / len(pieces), high / len(pieces))
        return jnp.repeat(jnp.exp(steps), dims[dim] // shards_of).reshape((-1,) + (1,) * (len(dims) - dim - 1))

    gain = one(*pieces[0])
    for cut in pieces[1:]:
        gain = gain * one(*cut)
    return gain


def profile(number_of, total, most, lean):
    portions = [(1 << 20) // math.isqrt(rank ** lean) + 1 for rank in range(2, number_of + 1)]
    surplus, counts = total - most - (number_of - 1), [1] * (number_of - 1)
    while surplus > 0:
        movable = [i for i in range(number_of - 1) if counts[i] < most]
        pool, remaining = sum([portions[i] for i in movable]), surplus
        for i in movable:
            addition = min(most - counts[i], max(1, remaining * portions[i] // pool), surplus)
            counts[i] = counts[i] + addition
            surplus = surplus - addition
    return np.array([most] + counts)


def ragged(key, amount, total, bound, slope):
    if amount == 2:
        one = jax.random.randint(key, (), max(1, total - bound), min(bound, total - 1) + 1)
        return jnp.stack([one, total - one])
    sizes = jnp.asarray(profile(amount, total, bound, slope), jnp.int32)
    pairs = (amount - 1) // 2
    giver, taker = sizes[1:1 + 2 * pairs:2], sizes[2:2 + 2 * pairs:2]
    room = jnp.minimum(giver - 1, bound - taker)
    moved = jax.random.randint(jax.random.fold_in(key, 1), (pairs,), 0, 1 << 20) % (room + 1)
    sizes = sizes.at[1:1 + 2 * pairs:2].set(giver - moved).at[2:2 + 2 * pairs:2].set(taker + moved)
    return sizes[jax.random.permutation(jax.random.fold_in(key, 2), amount)]


def deal_out(key, own, number, rows, amount, top, bound, slope):
    ranking = jax.random.permutation(key, amount)
    crowded, common = portions_of(amount, rows * top, bound, slope, True), portions_of(amount, rows * top, bound, slope, False)
    places = jnp.arange(amount)

    def named(sizes, offset_by):
        used = int((sizes > 0).sum())
        fixed = max(1, used // 4)
        shifted = fixed + (places - fixed + offset_by * (used - fixed)) % max(1, amount - fixed)
        return jnp.zeros((amount,), jnp.int32).at[ranking[jnp.where(places < fixed, places, shifted)]].set(jnp.asarray(sizes, jnp.int32))

    sizes = jnp.where(number % 4 == 0, named(crowded, number // 4), named(common, number - number // 4 - 1))
    mixed = jax.random.permutation(jax.random.fold_in(own, 3), amount)
    source_of, taker = mixed[0:amount // 2 * 2:2], mixed[1:amount // 2 * 2:2]
    slack = jnp.minimum(sizes[source_of] - 1, bound - sizes[taker]) // 2
    slack = jnp.where((source_of == ranking[0]) | (taker == ranking[0]) | (sizes[taker] == 0), 0, jnp.maximum(slack, 0))
    shifted = jax.random.randint(jax.random.fold_in(own, 4), (amount // 2,), 0, 1 << 20) % (slack + 1)
    sizes = sizes.at[source_of].add(-shifted).at[taker].add(shifted)
    members = jnp.searchsorted(jnp.cumsum(sizes), jnp.arange(rows * top), side="right").astype(jnp.int32)
    table = members.reshape(top, rows).T
    table = table[jax.random.permutation(jax.random.fold_in(own, 1), rows)]
    offset_by = jax.random.randint(jax.random.fold_in(own, 2), (rows, 1), 0, top)
    return jnp.take_along_axis(table, (jnp.arange(top)[None, :] + offset_by) % top, axis=1)


def portions_of(count, total, bound, skew, full):
    weights = [(1 << 20) // math.isqrt(standing ** skew) + 1 for standing in range(1, count + 1)]
    largest = bound if full else min(bound, max(-(-total // count), total * weights[0] // sum(weights)))
    least = 1 if total - largest >= count - 1 else 0
    given, surplus = [largest] + [least] * (count - 1), total - largest - least * (count - 1)
    while surplus > 0:
        free = [i for i in range(1, count) if given[i] < largest] or [i for i in range(1, count) if given[i] < bound]
        mass, remaining = sum([weights[i] for i in free]), surplus
        for i in free:
            extra = min(bound - given[i], max(1, remaining * weights[i] // mass), surplus)
            given[i] = given[i] + extra
            surplus = surplus - extra
    return np.array(given)


def bell_draw(key, dims, scale, most, pieces=(), kind=jnp.bfloat16):
    gain = steps_of(key, dims, pieces, -0.22, 0.18) if pieces else 1.0
    drawn = jax.random.normal(key, dims, jnp.float32) * scale * gain
    return jnp.minimum(jnp.maximum(drawn, -most), most).astype(kind)


def setup_inputs(seed: int = 0) -> dict:
    streams_of = jax.random.split(jax.random.key(seed), 11)
    inputs = bell_draw(streams_of[0], (STREAM_TOTAL, STREAM_SPAN, D), 1.0, 6.0, ((0, 16), (1, 8)))
    b_proj = bell_draw(streams_of[1], (STREAM_TOTAL, STREAM_SPAN, N), (N * BLOCK) ** -0.5, 0.046875, ((0, 16), (1, 8)))
    c_proj = bell_draw(streams_of[2], (STREAM_TOTAL, STREAM_SPAN, N), 1.0, 6.0, ((0, 16), (1, 8)))
    log_decay = draw_log_decay(jax.random.fold_in(streams_of[10], 71), 0)
    doc_lengths = jax.vmap(lambda own: ragged(own, DOCS, STREAM_SPAN, STREAM_SPAN // 2, 1))(jax.random.split(streams_of[4], STREAM_TOTAL)).reshape((STREAM_TOTAL, DOCS)).astype(jnp.int32)
    expert_ids_keys = jax.random.split(jax.random.fold_in(streams_of[5], 1), STREAM_TOTAL * STREAM_SPAN // TOK_DEV)
    expert_ids_turns = jax.random.permutation(jax.random.fold_in(streams_of[5], 3), STREAM_TOTAL * STREAM_SPAN // TOK_DEV)
    expert_ids = jax.vmap(lambda own, number: deal_out(jax.random.fold_in(streams_of[5], 2), own, number, TOK_DEV, EXPERTS, 2, CAP, 2))(expert_ids_keys, expert_ids_turns).reshape((STREAM_TOTAL, STREAM_SPAN, 2))
    gate_weights = jnp.clip(0.2 + 0.8 * jax.random.uniform(streams_of[6], (STREAM_TOTAL, STREAM_SPAN, 2), jnp.float32) ** steps_of(streams_of[6], (STREAM_TOTAL, STREAM_SPAN, 2), ((0, 16), (1, 8)), -0.2, 0.2), 0.2, 1.0)
    w_up = bell_draw(streams_of[7], (EXPERTS, D, HID), D ** -0.5, 0.09375, ((0, 16),))
    w_down = bell_draw(streams_of[8], (EXPERTS, HID, D), HID ** -0.5, 0.1875, ((0, 16),))
    cotangent = bell_draw(streams_of[9], (STREAM_TOTAL, STREAM_SPAN, D), 1.0, 6.0, ((0, 16), (1, 8)))
    return dict(inputs=inputs, b_proj=b_proj, c_proj=c_proj, log_decay=log_decay, doc_lengths=doc_lengths, expert_ids=expert_ids, gate_weights=gate_weights, w_up=w_up, w_down=w_down, cotangent=cotangent)


EPSILON = 1e-06
HIGHEST_PREC = lax.Precision.HIGHEST

def doc_index(starts, element_offsets):
    return lax.optimization_barrier(jnp.sum((starts[None, :] <= element_offsets[:, None]).astype(jnp.int32), axis=1)) - 1

def chain_states(retained, terms, backward):
    block_count = retained.shape[0]

    def advance(index, carry):
        state, stored = carry
        where_now = block_count - 1 - index if backward else index
        stored = lax.dynamic_update_index_in_dim(stored, state, where_now, 0)
        decay_now = lax.dynamic_index_in_dim(retained, where_now, 0, keepdims=False)
        term_now = lax.dynamic_index_in_dim(terms, where_now, 0, keepdims=False)
        state = decay_now[:, None, None] * state + term_now
        return (state, stored)
    start_state = jnp.zeros_like(terms[0])
    _, stored = lax.fori_loop(0, block_count, advance, (start_state, jnp.zeros_like(terms)))
    return stored

def block_terms(x_blocks, b_blocks, c_blocks, log_blocks, doc_of, doc_before):
    span_len = log_blocks.shape[2]
    cumulative = jnp.cumsum(log_blocks, axis=2)
    lower = jnp.arange(span_len)[:, None] >= jnp.arange(span_len)[None, :]
    same_doc = (doc_of[:, :, None] == doc_of[:, None, :]) & lower[None]
    spread = cumulative[:, :, :, None] - cumulative[:, :, None, :]
    decay_pairs = jnp.where(same_doc[:, None], jnp.exp(jnp.minimum(spread, 0.0)), 0.0)
    scores = jnp.einsum('ktn,ksn->kts', c_blocks.astype(jnp.float32), b_blocks.astype(jnp.float32), precision=HIGHEST_PREC)
    mixing = (decay_pairs * scores[:, None]).astype(jnp.bfloat16)
    opened = (doc_of == doc_before[:, None]).astype(jnp.float32)
    tail_mask = (doc_of == doc_of[:, -1:]).astype(jnp.float32)
    last_cum = cumulative[:, :, -1:]
    c_weighted = (opened[:, None, :, None] * jnp.exp(cumulative)[..., None] * c_blocks[:, None].astype(jnp.float32)).astype(jnp.bfloat16)
    b_weighted = (tail_mask[:, None, :, None] * jnp.exp(last_cum - cumulative)[..., None] * b_blocks[:, None].astype(jnp.float32)).astype(jnp.bfloat16)
    retained = opened[:, -1:] * jnp.exp(last_cum[:, :, 0])
    local_state = jnp.einsum('kshp,khsn->khpn', x_blocks.astype(jnp.float32), b_weighted.astype(jnp.float32), precision=HIGHEST_PREC)
    return (mixing, c_weighted, b_weighted, retained, local_state)

def sequence_blocks(x_seq, b_seq, c_seq, log_seq, lengths):
    block_count = STREAM_SPAN // BLOCK
    starts = (jnp.cumsum(lengths) - lengths).astype(jnp.int32)
    doc_of = doc_index(starts, jnp.arange(STREAM_SPAN, dtype=jnp.int32)).reshape(block_count, BLOCK)
    doc_before = doc_index(starts, jnp.arange(block_count, dtype=jnp.int32) * BLOCK - 1)
    x_blocks = x_seq.reshape(block_count, BLOCK, H, P_SIZE)
    log_blocks = log_seq.reshape(H, block_count, BLOCK).transpose(1, 0, 2)
    terms = block_terms(x_blocks, b_seq.reshape(block_count, BLOCK, N), c_seq.reshape(block_count, BLOCK, N), log_blocks, doc_of, doc_before)
    return (x_blocks, terms)

def sequence_forward(x_seq, b_seq, c_seq, log_seq, lengths):
    x_blocks, terms = sequence_blocks(x_seq, b_seq, c_seq, log_seq, lengths)
    mixing, c_weighted, b_weighted, retained, local_state = terms
    state_in = chain_states(retained, local_state, False)
    inner = jnp.einsum('khts,kshp->kthp', mixing.astype(jnp.float32), x_blocks.astype(jnp.float32), precision=HIGHEST_PREC)
    carried = jnp.einsum('khpn,khtn->kthp', state_in, c_weighted.astype(jnp.float32), precision=HIGHEST_PREC)
    return (inner + carried).astype(jnp.bfloat16).reshape(STREAM_SPAN, D)

def sequence_backward(x_seq, b_seq, c_seq, log_seq, lengths, grad_seq):
    x_blocks, terms = sequence_blocks(x_seq, b_seq, c_seq, log_seq, lengths)
    mixing, c_weighted, b_weighted, retained, local_state = terms
    block_count = STREAM_SPAN // BLOCK
    grad_blocks = grad_seq.reshape(block_count, BLOCK, H, P_SIZE).astype(jnp.float32)
    sources = jnp.einsum('kthp,khtn->khpn', grad_blocks, c_weighted.astype(jnp.float32), precision=HIGHEST_PREC)
    state_after = chain_states(retained, sources, True)
    inner = jnp.einsum('khts,kthp->kshp', mixing.astype(jnp.float32), grad_blocks, precision=HIGHEST_PREC)
    carried = jnp.einsum('khpn,khsn->kshp', state_after, b_weighted.astype(jnp.float32), precision=HIGHEST_PREC)
    return (inner + carried).astype(jnp.bfloat16).reshape(STREAM_SPAN, D)

def expert_rows(rows_in, rows_grad, expert_up, expert_down):
    pre_act = jnp.dot(rows_in, expert_up, preferred_element_type=jnp.float32)
    gate_sig = jax.nn.sigmoid(pre_act)
    activated = (pre_act * gate_sig).astype(jnp.bfloat16)
    expert_out = jnp.dot(activated, expert_down, preferred_element_type=jnp.float32).astype(jnp.bfloat16)
    back_hidden = jnp.dot(rows_grad, expert_down.T, preferred_element_type=jnp.float32)
    pre_grad = (back_hidden * gate_sig * (1.0 + pre_act * (1.0 - gate_sig))).astype(jnp.bfloat16)
    expert_grad = jnp.dot(pre_grad, expert_up.T, preferred_element_type=jnp.float32).astype(jnp.bfloat16)
    return (expert_out, expert_grad)

def reference(inputs, b_proj, c_proj, log_decay, doc_lengths, expert_ids, gate_weights, w_up, w_down, cotangent):
    resid = jnp.stack([sequence_forward(inputs[s], b_proj[s], c_proj[s], log_decay[s], doc_lengths[s]) for s in range(STREAM_TOTAL)])
    resid_rows = resid.reshape(-1, D).astype(jnp.float32)
    scale_rows = lax.rsqrt(lax.optimization_barrier(jnp.mean(resid_rows * resid_rows, axis=1, keepdims=True)) + EPSILON)
    normed = resid_rows * scale_rows
    mixed_in = normed.astype(jnp.bfloat16)
    grad_rows = cotangent.reshape(-1, D)
    expert_flat = expert_ids.reshape(-1)
    weight_flat = gate_weights.reshape(-1)
    slot_total = expert_flat.shape[0]
    row_bound = CAP * N_EXP * N_SEQ

    def per_expert(accumulated, expert_number):
        picked_rows = jnp.nonzero(expert_flat == expert_number, size=row_bound, fill_value=slot_total)[0].astype(jnp.int32)
        valid_rows = picked_rows < slot_total
        token_rows = jnp.where(valid_rows, picked_rows // 2, 0)
        weight_pick = jnp.where(valid_rows, weight_flat[jnp.minimum(picked_rows, slot_total - 1)], 0.0)[:, None]
        expert_out, expert_grad = expert_rows(mixed_in[token_rows], grad_rows[token_rows], w_up[expert_number], w_down[expert_number])
        moe_sum = accumulated[0].at[token_rows].add(weight_pick * expert_out.astype(jnp.float32))
        grad_sum = accumulated[1].at[token_rows].add(weight_pick * expert_grad.astype(jnp.float32))
        return ((moe_sum, grad_sum), None)
    zero_rows = jnp.zeros_like(resid_rows)
    (moe_rows, dmixed), _ = lax.scan(per_expert, (zero_rows, zero_rows), jnp.arange(EXPERTS, dtype=jnp.int32))
    output = (resid_rows + moe_rows).astype(jnp.bfloat16).reshape(STREAM_TOTAL, STREAM_SPAN, D)
    dresid = (grad_rows.astype(jnp.float32) + scale_rows * (dmixed - normed * lax.optimization_barrier(jnp.mean(dmixed * normed, axis=1, keepdims=True)))).astype(jnp.bfloat16)
    dresid_seq = dresid.reshape(STREAM_TOTAL, STREAM_SPAN, D)
    input_grad = jnp.stack([sequence_backward(inputs[s], b_proj[s], c_proj[s], log_decay[s], doc_lengths[s], dresid_seq[s]) for s in range(STREAM_TOTAL)])
    return (output, input_grad)
```

```python
import functools
import jax
import jax.numpy as jnp
from jax import lax
from jax.experimental import pallas as pl
from jax.experimental.pallas import tpu as pltpu
from jax.sharding import PartitionSpec as P

MESH = pl.DeviceIdType.MESH
F32, BF16, I32 = jnp.float32, jnp.bfloat16, jnp.int32
HIGHEST = lax.Precision.HIGHEST
EPSILON = 1e-06

T = 128
D = 4096
HID = 1024
H = 32
CAP = 24
SLOTS = 16 * CAP
NSEQ = 8
CHUNKS = 8
CW = D // CHUNKS
HALF = D // 2
VMEM_LIMIT = 62 * 1024 * 1024

NEAR = [(dx, dy) for dx in (0, 1, 3) for dy in (0, 1, 3) if (dx, dy) != (0, 0)]
FAR = [(dx, dy) for dx in range(4) for dy in range(4) if 2 in (dx, dy)]
ORDER = [(0, 0)] + NEAR + FAR


def code_row(d):
    return (d[1] * 4 + d[0]) * CAP


def slot_row(d):
    return ORDER.index(d) * CAP


def flip(d):
    return ((4 - d[0]) % 4, (4 - d[1]) % 4)


def place():
    me = lax.axis_index("exp")
    return lax.axis_index("seq"), lax.rem(me, 4), me // 4


def at(here, d):
    seq, x, y = here
    return (seq, lax.rem(y + d[1], 4) * 4 + lax.rem(x + d[0], 4))


def entry_barrier(here, with_chain):
    barrier = pltpu.get_barrier_semaphore()
    for d in NEAR:
        pl.semaphore_signal(barrier, inc=1, device_id=at(here, d), device_id_type=MESH)
    count = len(NEAR)
    if with_chain:
        for k in (1, NSEQ - 1):
            peer = (lax.rem(here[0] + k, NSEQ), lax.axis_index("exp"))
            pl.semaphore_signal(barrier, inc=1, device_id=peer, device_id_type=MESH)
        count += 2
    pl.semaphore_wait(barrier, count)


EXCHANGE_SEMS = [
    pltpu.SemaphoreType.DMA((2, len(NEAR))),
    pltpu.SemaphoreType.DMA((2, len(FAR), 2)),
    pltpu.SemaphoreType.DMA((2, len(FAR), 2)),
    pltpu.SemaphoreType.DMA((1,)),
]


class Exchange:
    def __init__(self, here, src, dst, stage, sems, back):
        near_sem, far_sem, fwd_sem, self_sem = sems
        src_row, dst_row = (slot_row, code_row) if back else (code_row, slot_row)

        def rows(ref, start):
            return ref.at[pl.ds(start, CAP)]

        self.own = pltpu.make_async_copy(
            rows(src, src_row((0, 0))), rows(dst, dst_row((0, 0))), self_sem.at[0]
        )
        self.near = {}
        for k, d in enumerate(NEAR):
            self.near[d] = pltpu.make_async_remote_copy(
                rows(src, src_row(d)),
                rows(dst, dst_row(d)),
                near_sem.at[0, k],
                near_sem.at[1, k],
                device_id=at(here, flip(d) if back else d),
                device_id_type=MESH,
            )
        self.far, self.fwd = ([], [])
        for j, d in enumerate(FAR):
            v = flip(d) if back else d
            for q, sign in enumerate((1, 3)):
                leg = tuple(sign if a == 2 else a for a in v)
                rest = tuple((a - b) % 4 for a, b in zip(v, leg))
                cols = pl.ds(q * HALF, HALF)
                self.far.append(
                    pltpu.make_async_remote_copy(
                        src.at[pl.ds(src_row(d), CAP), cols],
                        stage.at[j, q],
                        far_sem.at[0, j, q],
                        far_sem.at[1, j, q],
                        device_id=at(here, leg),
                        device_id_type=MESH,
                    )
                )
                self.fwd.append(
                    pltpu.make_async_remote_copy(
                        stage.at[j, q],
                        dst.at[pl.ds(dst_row(d), CAP), cols],
                        fwd_sem.at[0, j, q],
                        fwd_sem.at[1, j, q],
                        device_id=at(here, rest),
                        device_id_type=MESH,
                    )
                )

    def start_far(self):
        for c in self.far:
            c.start()

    def start_near(self, which):
        for d in which:
            if d == (0, 0):
                self.own.start()
            else:
                self.near[d].start()

    def forward(self):
        for c, f in zip(self.far, self.fwd):
            c.wait_recv()
            f.start()

    def wait_near(self, which):
        for d in which:
            if d == (0, 0):
                self.own.wait()
            else:
                self.near[d].wait_recv()

    def wait_far(self):
        for f in self.fwd:
            f.wait_recv()

    def finish(self):
        for c in list(self.near.values()) + self.far + self.fwd:
            c.wait_send()


def iota(shape, dim):
    return lax.broadcasted_iota(I32, shape, dim)


def nt(a, b, precision=None):
    return lax.dot_general(
        a, b, (((1,), (1,)), ((), ())), precision=precision, preferred_element_type=F32
    )


def nn(a, b, precision=None):
    return jnp.dot(a, b, precision=precision, preferred_element_type=F32)


def slot_columns(ids_ref, here):
    seq, x, y = here
    codes = []
    for j in range(2):
        e = ids_ref[:, j : j + 1]
        codes.append((((e // 4) - y) & 3) * 4 + ((e & 3) - x & 3))
    lane = iota((T, T), 1)
    named = [lane == code for code in codes]
    both = jnp.where(named[0] | named[1], 1.0, 0.0).astype(BF16)
    earlier = jnp.where(iota((T, T), 1) < iota((T, T), 0), 1.0, 0.0).astype(BF16)
    rank = nn(earlier, both)
    return [
        code * CAP + jnp.sum(jnp.where(n, rank, 0.0), axis=1, keepdims=True).astype(I32)
        for code, n in zip(codes, named)
    ]


def pick_matrix(slots):
    eye = iota((T, T), 0) == iota((T, T), 1)
    s = iota((SLOTS, T), 0)
    hit = None
    for slot in slots:
        row = jnp.sum(jnp.where(eye, slot, 0), axis=0, keepdims=True)
        hit = (s == row) if hit is None else hit | (s == row)
    return jnp.where(hit, 1.0, 0.0).astype(BF16)


def weight_matrices(slots, gate_ref):
    s = iota((T, SLOTS), 1)
    w = jnp.zeros((T, SLOTS), F32)
    for j, slot in enumerate(slots):
        w = w + jnp.where(s == slot, gate_ref[:, j : j + 1], 0.0)
    high = w.astype(BF16)
    return high, (w - high.astype(F32)).astype(BF16)


def doc_facts(len_ref, seq):
    base = seq * T
    starts = [jnp.int32(0)]
    for j in range(5):
        starts.append(starts[-1] + len_ref[0, j])

    def doc(pos):
        total = jnp.where(starts[0] <= pos, 1, 0)
        for s in starts[1:]:
            total = total + jnp.where(s <= pos, 1, 0)
        return total - 1

    row, col = doc(base + iota((1, T), 1)), doc(base + iota((T, 1), 0))
    return row, col, doc(base - 1), doc(base + T - 1)


def local_terms(fwd, facts, ld_ref, b, c, rhs_ref, inner_ref, local_ref, col_ref, kept_ref):
    doc_row, doc_col, before, last_doc = facts
    down, across = iota((T, T), 0), iota((T, T), 1)
    own, other = (c, b) if fwd else (b, c)
    causal = (down >= across) if fwd else (across >= down)
    scores = jnp.where(causal & (doc_col == doc_row), nt(own, other), 0.0)
    eye = jnp.where(down == across, 1.0, 0.0).astype(BF16)
    turned = nt(eye, other)
    upto = jnp.where(down <= across, 1.0, 0.0)
    upto_t = jnp.where(across <= down, 1.0, 0.0)
    opened_e = jnp.where(last_doc == before, 1.0, 0.0)
    if fwd:
        row_mask = jnp.where(doc_row == last_doc, 1.0, 0.0)
        col_mask = jnp.where(doc_col == before, 1.0, 0.0)
    else:
        row_mask = jnp.where(doc_row == before, 1.0, 0.0)
        col_mask = jnp.where(doc_col == last_doc, 1.0, 0.0)

    def group(g, _):
        ld = ld_ref[pl.ds(pl.multiple_of(g * 8, 8), 8), :]
        crow = nn(ld, upto, HIGHEST)
        ccol = nt(upto_t, ld, HIGHEST)
        last = crow[:, T - 1 : T]
        if fwd:
            frow = row_mask * jnp.exp(last - crow)
            gcol = col_mask * jnp.exp(ccol)
        else:
            frow = row_mask * jnp.exp(crow)
            gcol = col_mask * jnp.exp(ccol[T - 1 : T, :] - ccol)
        col_ref[g] = gcol
        kept = opened_e * jnp.exp(last)
        for h in range(8):
            spread = ccol[:, h : h + 1] - crow[h : h + 1, :]
            if not fwd:
                spread = -spread
            pair = (jnp.exp(jnp.minimum(spread, 0.0)) * scores).astype(BF16)
            weighted = (turned * frow[h : h + 1, :]).astype(BF16)
            cols = pl.ds(pl.multiple_of(g * 8 * T, 8 * T) + h * T, T)
            both = nn(jnp.concatenate([pair, weighted], axis=0), rhs_ref[:, cols])
            inner_ref[:, cols] = both[:T]
            part = slice((h % 4) * T, (h % 4 + 1) * T)
            local_ref[g * 2 + h // 4, :, part] = both[T:]
            kept_ref[g * 2 + h // 4, :, part] = jnp.broadcast_to(kept[h : h + 1, :], (8, T))
        return 0

    lax.fori_loop(0, H // 8, group, 0)


def chain(
    fwd, here, exchange, proj, inner_ref, local_ref, col_ref, kept_ref,
    in_buf, out_buf, chain_sem, emit,
):
    seq = here[0]
    first, final = (0, NSEQ - 1) if fwd else (NSEQ - 1, 0)
    depth = seq if fwd else NSEQ - 1 - seq
    peer = (lax.rem(seq + (1 if fwd else NSEQ - 1), NSEQ), lax.axis_index("exp"))

    @pl.when(depth >= NSEQ // 2)
    def _():
        exchange.forward()

    @pl.when(seq == first)
    def _():
        in_buf[...] = jnp.zeros_like(in_buf)

    copies = []
    for k in range(CHUNKS):
        copy = pltpu.make_async_remote_copy(
            out_buf.at[k], in_buf.at[k], chain_sem.at[0, k], chain_sem.at[1, k],
            device_id=peer, device_id_type=MESH,
        )
        copies.append(copy)

        @pl.when(seq != first)
        def _():
            copy.wait_recv()

        state = in_buf[k]

        @pl.when(seq != final)
        def _():
            out_buf[k] = (kept_ref[k, 0:1, :] * state.astype(F32) + local_ref[k]).astype(BF16)
            copy.start()

        carried = nn(proj, state)
        gcol = col_ref[k // 2]
        for h in range(4):
            cols = slice(k * CW + h * T, k * CW + (h + 1) * T)
            j = (k % 2) * 4 + h
            emit(cols, inner_ref[:, cols] + gcol[:, j : j + 1] * carried[:, h * T : (h + 1) * T])

    @pl.when(depth < NSEQ // 2)
    def _():
        exchange.forward()

    @pl.when(seq != final)
    def _():
        for copy in copies:
            copy.wait_send()


def forward_kernel(
    len_ref, x_ref, b_ref, c_ref, ld_ref, ids_ref, cot_ref,
    resid_ref, sent_ref, got_ref, stage_ref, send_ref,
    packed, inner, local, colw, kept, in_buf, out_buf, chain_sem, put_sem, *sems,
):
    here = place()
    exchange = Exchange(here, send_ref, got_ref, stage_ref, sems, False)
    pick = pick_matrix(slot_columns(ids_ref, here))

    def gather(n, _):
        cols = pl.ds(pl.multiple_of(n * CW, CW), CW)
        packed[:, cols] = nn(pick, cot_ref[:, cols]).astype(BF16)
        return 0

    lax.fori_loop(0, D // CW, gather, 0)
    put = pltpu.make_async_copy(packed, send_ref, put_sem.at[0])
    put.start()
    entry_barrier(here, True)
    put.wait()
    exchange.start_far()
    exchange.start_near(ORDER[:9])

    c = c_ref[...]
    facts = doc_facts(len_ref, here[0])
    local_terms(True, facts, ld_ref, b_ref[...], c, x_ref, inner, local, colw, kept)

    def emit(cols, value):
        resid_ref[:, cols] = value.astype(BF16)

    chain(
        True, here, exchange, c, inner, local, colw, kept, in_buf, out_buf, chain_sem, emit
    )
    total = jnp.zeros((T, CW), F32)
    for k in range(CHUNKS):
        rows = resid_ref[:, k * CW : (k + 1) * CW].astype(F32)
        total = total + rows * rows
    scale = lax.rsqrt(jnp.sum(total, axis=1, keepdims=True) / D + EPSILON)

    def gather_mixed(n, _):
        cols = pl.ds(pl.multiple_of(n * CW, CW), CW)
        mixed = (resid_ref[:, cols].astype(F32) * scale).astype(BF16)
        sent_ref[:, cols] = nn(pick, mixed).astype(BF16)
        return 0

    lax.fori_loop(0, D // CW, gather_mixed, 0)
    exchange.wait_near(ORDER[:9])
    exchange.wait_far()
    exchange.finish()


GROUP = SLOTS // 2
HTILE = 256
FTILE = 512


def expert_kernel(
    sent_ref, cot_ref, wu_hbm, wd_hbm,
    got_ref, out_ref, recv_ref, stage_ref, stage2_ref, grad_ref,
    wu, wd, cot, rows, back, act, pre_grad, packed, load_sem, *sems,
):
    here = place()
    there = Exchange(here, sent_ref, recv_ref, stage_ref, sems[:4], False)
    home = Exchange(here, grad_ref, got_ref, stage2_ref, sems[4:], True)
    loads = [
        pltpu.make_async_copy(s, d, load_sem.at[k])
        for k, (s, d) in enumerate([(cot_ref, cot), (wd_hbm, wd), (wu_hbm, wu)])
    ]
    for load in loads:
        load.start()
    entry_barrier(here, False)
    there.start_far()
    there.start_near(ORDER[:9])
    loads[0].wait()
    loads[1].wait()

    def back_tile(n, _):
        part = pl.ds(pl.multiple_of(n * HTILE, HTILE), HTILE)
        back[:, part] = nt(cot[...], wd[part, :])
        return 0

    lax.fori_loop(0, HID // HTILE, back_tile, 0)
    loads[2].wait()
    there.forward()

    puts = []
    for g in range(2):
        group = pl.ds(g * GROUP, GROUP)
        if g == 0:
            there.wait_near(ORDER[:8])
        else:
            there.wait_near(ORDER[8:9])
            there.wait_far()
        load = pltpu.make_async_copy(recv_ref.at[group], rows.at[g], load_sem.at[3 + g])
        load.start()
        load.wait()

        def up_tile(n, _):
            part = pl.ds(pl.multiple_of(n * HTILE, HTILE), HTILE)
            pre = nn(rows[g], wu[:, part])
            sig = 1.0 / (1.0 + jnp.exp(-pre))
            act[group, part] = (pre * sig).astype(BF16)
            pre_grad[group, part] = (
                back[group, part] * sig * (1.0 + pre * (1.0 - sig))
            ).astype(BF16)
            return 0

        lax.fori_loop(0, HID // HTILE, up_tile, 0)

        def grad_tile(n, _):
            part = pl.ds(pl.multiple_of(n * FTILE, FTILE), FTILE)
            packed[group, part] = nt(pre_grad[group, :], wu[part, :]).astype(BF16)
            return 0

        lax.fori_loop(0, D // FTILE, grad_tile, 0)
        put = pltpu.make_async_copy(packed.at[group], grad_ref.at[group], load_sem.at[5 + g])
        put.start()
        put.wait()
        if g == 0:
            home.start_near(ORDER[:8])
        else:
            home.start_far()
            home.start_near(ORDER[8:9])

    def out_tile(n, _):
        part = pl.ds(pl.multiple_of(n * FTILE, FTILE), FTILE)
        packed[:, part] = nn(act[...], wd[:, part]).astype(BF16)
        return 0

    lax.fori_loop(0, D // FTILE, out_tile, 0)
    put = pltpu.make_async_copy(packed, out_ref, load_sem.at[7])
    put.start()
    home.forward()
    put.wait()
    home.wait_near(ORDER[:9])
    home.wait_far()
    home.finish()
    there.finish()


def backward_kernel(
    len_ref, grad_ref, send_ref, resid_ref, cot_ref, b_ref, c_ref, ld_ref, ids_ref, gate_ref,
    output_ref, dx_ref, got_ref, stage_ref,
    dres, got, inner, local, colw, kept, in_buf, out_buf, chain_sem, load_sem, *sems,
):
    here = place()
    exchange = Exchange(here, send_ref, got_ref, stage_ref, sems, True)
    entry_barrier(here, True)
    exchange.start_far()
    exchange.start_near(ORDER[:9])
    high, low = weight_matrices(slot_columns(ids_ref, here), gate_ref)
    total = jnp.zeros((T, CW), F32)
    for k in range(CHUNKS):
        rows = resid_ref[:, k * CW : (k + 1) * CW].astype(F32)
        total = total + rows * rows
    scale = lax.rsqrt(jnp.sum(total, axis=1, keepdims=True) / D + EPSILON)

    def combine(n, total):
        cols = pl.ds(pl.multiple_of(n * CW, CW), CW)
        dmixed = nn(high, grad_ref[:, cols]) + nn(low, grad_ref[:, cols])
        inner[:, cols] = dmixed
        return total + dmixed * (resid_ref[:, cols].astype(F32) * scale)

    total = lax.fori_loop(0, D // CW, combine, jnp.zeros((T, CW), F32))
    mean = jnp.sum(total, axis=1, keepdims=True) / D

    def finish_rows(n, _):
        cols = pl.ds(pl.multiple_of(n * CW, CW), CW)
        normed = resid_ref[:, cols].astype(F32) * scale
        dres[:, cols] = (
            cot_ref[:, cols].astype(F32) + scale * (inner[:, cols] - normed * mean)
        ).astype(BF16)
        return 0

    lax.fori_loop(0, D // CW, finish_rows, 0)
    b = b_ref[...]
    facts = doc_facts(len_ref, here[0])
    local_terms(False, facts, ld_ref, b, c_ref[...], dres, inner, local, colw, kept)

    def emit(cols, value):
        dx_ref[:, cols] = value.astype(BF16)

    chain(
        False, here, exchange, b, inner, local, colw, kept, in_buf, out_buf, chain_sem, emit
    )
    exchange.wait_near(ORDER[:9])
    exchange.wait_far()
    load = pltpu.make_async_copy(got_ref, got, load_sem.at[0])
    load.start()
    load.wait()

    def combine_out(n, _):
        cols = pl.ds(pl.multiple_of(n * CW, CW), CW)
        moe = nn(high, got[:, cols]) + nn(low, got[:, cols])
        output_ref[:, cols] = (resid_ref[:, cols].astype(F32) + moe).astype(BF16)
        return 0

    lax.fori_loop(0, D // CW, combine_out, 0)
    exchange.finish()


VM = pl.BlockSpec(memory_space=pltpu.VMEM)
SM = pl.BlockSpec(memory_space=pltpu.SMEM)
HB = pl.BlockSpec(memory_space=pltpu.HBM)
ROWS = jax.ShapeDtypeStruct((SLOTS, D), BF16)
STAGE = jax.ShapeDtypeStruct((len(FAR), 2, CAP, HALF), BF16)
TOKENS = jax.ShapeDtypeStruct((T, D), BF16)
SSD_SCRATCH = [
    pltpu.VMEM((T, D), F32),
    pltpu.VMEM((CHUNKS, T, CW), F32),
    pltpu.VMEM((H // 8, T, 8), F32),
    pltpu.VMEM((CHUNKS, 8, CW), F32),
    pltpu.VMEM((CHUNKS, T, CW), BF16),
    pltpu.VMEM((CHUNKS, T, CW), BF16),
    pltpu.SemaphoreType.DMA((2, CHUNKS)),
]


def call(kernel, ident, ins, outs, out_specs, scratch):
    return pl.pallas_call(
        kernel,
        out_shape=outs,
        in_specs=ins,
        out_specs=out_specs,
        scratch_shapes=scratch,
        compiler_params=pltpu.CompilerParams(
            collective_id=ident, has_side_effects=True, vmem_limit_bytes=VMEM_LIMIT
        ),
    )


def on_device(
    inputs, b_proj, c_proj, log_decay, doc_lengths, expert_ids, gate_weights, w_up, w_down,
    cotangent,
):
    x, b, c, ld, ids = (inputs[0], b_proj[0], c_proj[0], log_decay[0], expert_ids[0])
    resid, sent, got_cot, _, _ = call(
        forward_kernel, 1,
        [SM] + [VM] * 6,
        [TOKENS, ROWS, ROWS, STAGE, ROWS],
        [VM, VM, HB, HB, HB],
        [pltpu.VMEM((SLOTS, D), BF16)]
        + SSD_SCRATCH
        + [pltpu.SemaphoreType.DMA((1,))]
        + EXCHANGE_SEMS,
    )(doc_lengths, x, b, c, ld, ids, cotangent[0])
    got_grad, out_rows, _, _, _, _ = call(
        expert_kernel, 2,
        [HB] * 4,
        [ROWS, ROWS, ROWS, STAGE, STAGE, ROWS],
        [HB] * 6,
        [
            pltpu.VMEM((D, HID), BF16),
            pltpu.VMEM((HID, D), BF16),
            pltpu.VMEM((SLOTS, D), BF16),
            pltpu.VMEM((2, GROUP, D), BF16),
            pltpu.VMEM((SLOTS, HID), F32),
            pltpu.VMEM((SLOTS, HID), BF16),
            pltpu.VMEM((SLOTS, HID), BF16),
            pltpu.VMEM((SLOTS, D), BF16),
            pltpu.SemaphoreType.DMA((8,)),
        ]
        + EXCHANGE_SEMS * 2,
    )(sent, got_cot, w_up[0], w_down[0])
    output, dx, _, _ = call(
        backward_kernel, 3,
        [SM, VM, HB] + [VM] * 7,
        [TOKENS, TOKENS, ROWS, STAGE],
        [VM, VM, HB, HB],
        [pltpu.VMEM((T, D), BF16), pltpu.VMEM((SLOTS, D), BF16)]
        + SSD_SCRATCH
        + [pltpu.SemaphoreType.DMA((1,))]
        + EXCHANGE_SEMS,
    )(
        doc_lengths, got_grad, out_rows, resid, cotangent[0], b, c, ld, ids, gate_weights[0]
    )
    return (output[None], dx[None])


def solution(mesh):
    rows = P("exp", "seq", None)
    whole = P("exp", None, None)
    return jax.shard_map(
        on_device,
        mesh=mesh,
        in_specs=(
            rows, rows, rows, P("exp", None, "seq"), P("exp", None), rows, rows, whole, whole,
            rows,
        ),
        out_specs=(rows, rows),
        check_vma=False,
    )
```

```python
import functools
import jax
import jax.numpy as jnp
from jax import lax
from jax.experimental import pallas as pl
from jax.experimental.pallas import tpu as pltpu
from jax.sharding import PartitionSpec as P

MESH = pl.DeviceIdType.MESH
F32, BF16, I32 = jnp.float32, jnp.bfloat16, jnp.int32
HIGHEST = lax.Precision.HIGHEST
EPSILON = 1e-06

T = 128
D = 4096
HID = 1024
H = 32
CAP = 24
SLOTS = 16 * CAP
NSEQ = 8
CHUNKS = 8
CW = D // CHUNKS
HALF = D // 2
VMEM_LIMIT = 62 * 1024 * 1024

NEAR = [(0, 1), (1, 0), (0, 3), (3, 0), (1, 1), (3, 3), (1, 3), (3, 1)]
FAR = [(dx, dy) for dx in range(4) for dy in range(4) if 2 in (dx, dy)]
ORDER = [(0, 0)] + NEAR + FAR


def code_row(d):
    return (d[1] * 4 + d[0]) * CAP


def slot_row(d):
    return ORDER.index(d) * CAP


def flip(d):
    return ((4 - d[0]) % 4, (4 - d[1]) % 4)


def place():
    me = lax.axis_index("exp")
    return lax.axis_index("seq"), lax.rem(me, 4), me // 4


def at(here, d):
    seq, x, y = here
    return (seq, lax.rem(y + d[1], 4) * 4 + lax.rem(x + d[0], 4))


def greet(here):
    barrier = pltpu.get_barrier_semaphore()
    for d in NEAR:
        pl.semaphore_signal(barrier, inc=1, device_id=at(here, d), device_id_type=MESH)
    for k in (1, NSEQ - 1):
        peer = (lax.rem(here[0] + k, NSEQ), lax.axis_index("exp"))
        pl.semaphore_signal(barrier, inc=1, device_id=peer, device_id_type=MESH)


def wait_for_all():
    pl.semaphore_wait(pltpu.get_barrier_semaphore(), len(NEAR) + 2)


EXCHANGE_SEMS = [
    pltpu.SemaphoreType.DMA((2, len(NEAR))),
    pltpu.SemaphoreType.DMA((2, len(FAR), 2)),
    pltpu.SemaphoreType.DMA((2, len(FAR), 2)),
    pltpu.SemaphoreType.DMA((1,)),
]


class Exchange:
    def __init__(self, here, src, dst, stage, sems, back):
        near_sem, far_sem, fwd_sem, self_sem = sems
        src_row, dst_row = (slot_row, code_row) if back else (code_row, slot_row)

        def rows(ref, start):
            return ref.at[pl.ds(start, CAP)]

        self.own = pltpu.make_async_copy(
            rows(src, src_row((0, 0))), rows(dst, dst_row((0, 0))), self_sem.at[0]
        )
        self.near = {}
        for k, d in enumerate(NEAR):
            self.near[d] = pltpu.make_async_remote_copy(
                rows(src, src_row(d)),
                rows(dst, dst_row(d)),
                near_sem.at[0, k],
                near_sem.at[1, k],
                device_id=at(here, flip(d) if back else d),
                device_id_type=MESH,
            )
        self.far, self.fwd = ([], [])
        for j, d in enumerate(FAR):
            v = flip(d) if back else d
            for q, sign in enumerate((1, 3) if j % 2 else (3, 1)):
                leg = tuple(sign if a == 2 else a for a in v)
                rest = tuple((a - b) % 4 for a, b in zip(v, leg))
                cols = pl.ds(q * HALF, HALF)
                self.far.append(
                    pltpu.make_async_remote_copy(
                        src.at[pl.ds(src_row(d), CAP), cols],
                        stage.at[j, q],
                        far_sem.at[0, j, q],
                        far_sem.at[1, j, q],
                        device_id=at(here, leg),
                        device_id_type=MESH,
                    )
                )
                self.fwd.append(
                    pltpu.make_async_remote_copy(
                        stage.at[j, q],
                        dst.at[pl.ds(dst_row(d), CAP), cols],
                        fwd_sem.at[0, j, q],
                        fwd_sem.at[1, j, q],
                        device_id=at(here, rest),
                        device_id_type=MESH,
                    )
                )

    def start_far(self, half):
        for c in self.far[half::2]:
            c.start()

    def start_near(self, which):
        for d in which:
            if d == (0, 0):
                self.own.start()
            else:
                self.near[d].start()

    def forward(self):
        for c, f in zip(self.far, self.fwd):
            c.wait_recv()
            f.start()

    def wait_near(self, which):
        for d in which:
            if d == (0, 0):
                self.own.wait()
            else:
                self.near[d].wait_recv()

    def wait_far(self):
        for f in self.fwd:
            f.wait_recv()

    def finish(self):
        for c in list(self.near.values()) + self.far + self.fwd:
            c.wait_send()


def iota(shape, dim):
    return lax.broadcasted_iota(I32, shape, dim)


def nt(a, b, precision=None):
    return lax.dot_general(
        a, b, (((1,), (1,)), ((), ())), precision=precision, preferred_element_type=F32
    )


def nn(a, b, precision=None):
    return jnp.dot(a, b, precision=precision, preferred_element_type=F32)


def to_column(row):
    eye = iota((T, T), 0) == iota((T, T), 1)
    return jnp.sum(jnp.where(eye, row, 0.0), axis=1, keepdims=True)


def slot_columns(ids_ref, here):
    seq, x, y = here
    codes = []
    for j in range(2):
        e = ids_ref[j : j + 1, :]
        code = (((e // 4) - y) & 3) * 4 + (((e & 3) - x) & 3)
        codes.append(to_column(code.astype(F32)).astype(I32))
    lane = iota((T, T), 1)
    named = [lane == code for code in codes]
    both = jnp.where(named[0] | named[1], 1.0, 0.0).astype(BF16)
    earlier = jnp.where(iota((T, T), 1) < iota((T, T), 0), 1.0, 0.0).astype(BF16)
    rank = nn(earlier, both)
    return [
        code * CAP + jnp.sum(jnp.where(n, rank, 0.0), axis=1, keepdims=True).astype(I32)
        for code, n in zip(codes, named)
    ]


def pick_matrix(slots):
    eye = iota((T, T), 0) == iota((T, T), 1)
    s = iota((SLOTS, T), 0)
    hit = None
    for slot in slots:
        row = jnp.sum(jnp.where(eye, slot, 0), axis=0, keepdims=True)
        hit = (s == row) if hit is None else hit | (s == row)
    return jnp.where(hit, 1.0, 0.0).astype(BF16)


def weight_matrices(slots, gate_ref):
    s = iota((T, SLOTS), 1)
    w = jnp.zeros((T, SLOTS), F32)
    for j, slot in enumerate(slots):
        w = w + jnp.where(s == slot, to_column(gate_ref[j : j + 1, :]), 0.0)
    high = w.astype(BF16)
    return high, (w - high.astype(F32)).astype(BF16)


def doc_facts(len_ref, seq):
    base = seq * T
    starts = [jnp.int32(0)]
    for j in range(5):
        starts.append(starts[-1] + len_ref[0, j])

    def doc(pos):
        total = jnp.where(starts[0] <= pos, 1, 0)
        for s in starts[1:]:
            total = total + jnp.where(s <= pos, 1, 0)
        return total - 1

    row, col = doc(base + iota((1, T), 1)), doc(base + iota((T, 1), 0))
    return row, col, doc(base - 1), doc(base + T - 1)


class Pass:
    def __init__(self, fwd, here, facts, ld_ref, b, c, rhs_ref, refs, in_buf, out_buf, sem):
        self.fwd, self.seq, self.ld_ref, self.rhs_ref = (fwd, here[0], ld_ref, rhs_ref)
        self.lhs, self.inner, self.local, self.colw, self.kept = refs
        self.in_buf, self.out_buf, self.sem = (in_buf, out_buf, sem)
        self.proj = c if fwd else b
        doc_row, doc_col, before, last_doc = facts
        down, across = iota((T, T), 0), iota((T, T), 1)
        other = b if fwd else c
        causal = (down >= across) if fwd else (across >= down)
        self.scores = jnp.where(causal & (doc_col == doc_row), nt(self.proj, other), 0.0)
        eye = jnp.where(down == across, 1.0, 0.0).astype(BF16)
        self.turned = nt(eye, other)
        self.upto = jnp.where(down <= across, 1.0, 0.0)
        self.upto_t = jnp.where(across <= down, 1.0, 0.0)
        self.opened_e = jnp.where(last_doc == before, 1.0, 0.0)
        row_doc, col_doc = (last_doc, before) if fwd else (before, last_doc)
        self.row_mask = jnp.where(doc_row == row_doc, 1.0, 0.0)
        self.col_mask = jnp.where(doc_col == col_doc, 1.0, 0.0)

    def prepare(self, g):
        ld = self.ld_ref[pl.ds(pl.multiple_of(g * 8, 8), 8), :]
        crow = nn(ld, self.upto, HIGHEST)
        ccol = nt(self.upto_t, ld, HIGHEST)
        last = crow[:, T - 1 : T]
        if self.fwd:
            frow = self.row_mask * jnp.exp(last - crow)
            self.colw[g] = self.col_mask * jnp.exp(ccol)
        else:
            frow = self.row_mask * jnp.exp(crow)
            self.colw[g] = self.col_mask * jnp.exp(ccol[T - 1 : T, :] - ccol)
        kept = self.opened_e * jnp.exp(last)
        for h in range(8):
            spread = ccol[:, h : h + 1] - crow[h : h + 1, :]
            if not self.fwd:
                spread = -spread
            pair = jnp.exp(jnp.minimum(spread, 0.0)) * self.scores
            self.lhs[g * 8 + h, :T, :] = pair.astype(BF16)
            self.lhs[g * 8 + h, T:, :] = (self.turned * frow[h : h + 1, :]).astype(BF16)
            part = slice((h % 4) * T, (h % 4 + 1) * T)
            self.kept[g * 2 + h // 4, :, part] = jnp.broadcast_to(kept[h : h + 1, :], (8, T))

    def apply(self, g):
        for h in range(8):
            cols = pl.ds(pl.multiple_of(g * 8 * T, 8 * T) + h * T, T)
            both = nn(self.lhs[g * 8 + h], self.rhs_ref[:, cols])
            self.inner[:, cols] = both[:T]
            part = slice((h % 4) * T, (h % 4 + 1) * T)
            self.local[g * 2 + h // 4, :, part] = both[T:]

    def run(self, group, forward, turns, emit):
        first, final = (0, NSEQ - 1) if self.fwd else (NSEQ - 1, 0)
        seq = self.seq
        depth = seq if self.fwd else NSEQ - 1 - seq
        step = 1 if self.fwd else NSEQ - 1
        peer = (lax.rem(seq + step, NSEQ), lax.axis_index("exp"))

        @pl.when(seq == first)
        def _():
            self.in_buf[...] = jnp.zeros_like(self.in_buf)

        @pl.when(seq != first)
        def _():
            def each(g, _):
                group(g)
                return 0

            lax.fori_loop(0, H // 8, each, 0)

        copies = []
        for k in range(CHUNKS + 1):
            depths = [d for d in range(NSEQ) if turns[d] == k]
            if depths:

                @pl.when((depth >= depths[0]) & (depth <= depths[-1]))
                def _():
                    forward()

            if k == CHUNKS:
                break
            if k % 2 == 0:

                @pl.when(seq == first)
                def _():
                    group(k // 2)

            copy = pltpu.make_async_remote_copy(
                self.out_buf.at[k], self.in_buf.at[k], self.sem.at[0, k], self.sem.at[1, k],
                device_id=peer, device_id_type=MESH,
            )
            copies.append(copy)

            @pl.when(seq != first)
            def _():
                copy.wait_recv()

            state = self.in_buf[k]

            @pl.when(seq != final)
            def _():
                handed = self.kept[k, 0:1, :] * state.astype(F32) + self.local[k]
                self.out_buf[k] = handed.astype(BF16)
                copy.start()

            carried = nn(self.proj, state)
            colw = self.colw[k // 2]
            for h in range(4):
                cols = slice(k * CW + h * T, k * CW + (h + 1) * T)
                j = (k % 2) * 4 + h
                state_term = colw[:, j : j + 1] * carried[:, h * T : (h + 1) * T]
                emit(cols, self.inner[:, cols] + state_term)

        @pl.when(seq != final)
        def _():
            for copy in copies:
                copy.wait_send()


GROUP = SLOTS // 2
HTILE = 256
FTILE = 512


def columns(n, width):
    return pl.ds(pl.multiple_of(n * width, width), width)


def gather_half(half, pick, packed, send_ref, put_sem, tile):
    def step(n, _):
        cols = columns(n, CW)
        packed[:, cols] = nn(pick, tile(cols)).astype(BF16)
        return 0

    lax.fori_loop(half * (HALF // CW), (half + 1) * (HALF // CW), step, 0)
    cols = pl.ds(half * HALF, HALF)
    put = pltpu.make_async_copy(packed.at[:, cols], send_ref.at[:, cols], put_sem)
    put.start()
    return put


def row_scale(resid):
    total = jnp.zeros((T, CW), F32)
    for k in range(CHUNKS):
        rows = resid[:, k * CW : (k + 1) * CW].astype(F32)
        total = total + rows * rows
    return lax.rsqrt(jnp.sum(total, axis=1, keepdims=True) / D + EPSILON)


def layer_kernel(
    len_ref, x_hbm, b_hbm, c_hbm, ld_hbm, ids_ref, gate_ref, wu_hbm, wd_hbm, cot_hbm,
    resid_hbm, dx_hbm, high_hbm, low_hbm, got4,
    send1, got1, stage1, send2, got2, stage2, send3, got3, stage3, send4, stage4,
    x_ref, cot_ref, b_ref, c_ref, ld_ref, resid, dres, dx_ref, high_ref, low_ref,
    packed, got, rows, wu, wd, back, act, pre_grad,
    lhs, inner, local, colw, kept, fwd_in, bwd_in, out_buf, chain_sem, load_sem, put_sem, *sems,
):
    here = place()
    first = Exchange(here, send1, got1, stage1, sems[0:4], False)
    second = Exchange(here, send2, got2, stage2, sems[4:8], False)
    third = Exchange(here, send3, got3, stage3, sems[8:12], True)
    fourth = Exchange(here, send4, got4, stage4, sems[12:16], True)

    def load(k, src, dst):
        copy = pltpu.make_async_copy(src, dst, load_sem.at[k])
        copy.start()
        return copy

    cot_load = load(0, cot_hbm, cot_ref)
    loads = [
        load(1 + k, s, d)
        for k, (s, d) in enumerate(
            [(x_hbm, x_ref), (b_hbm, b_ref), (c_hbm, c_ref), (ld_hbm, ld_ref)]
        )
    ]
    greet(here)
    slots = slot_columns(ids_ref, here)
    pick = pick_matrix(slots)
    cot_load.wait()

    puts = [
        gather_half(h, pick, packed, send1, put_sem.at[h], lambda cols: cot_ref[:, cols])
        for h in range(2)
    ]
    puts[0].wait()
    wait_for_all()
    first.start_far(0)
    puts[1].wait()
    first.start_far(1)
    first.start_near(ORDER[:9])
    wd_load = load(5, wd_hbm, wd)
    wu_load = load(6, wu_hbm, wu)
    for copy in loads:
        copy.wait()
    b, c = b_ref[...], c_ref[...]
    facts = doc_facts(len_ref, here[0])
    refs = (lhs, inner, local, colw, kept)
    ahead = Pass(
        True, here, facts, ld_ref, b, c, x_ref, refs, fwd_in, out_buf.at[0], chain_sem.at[0]
    )

    def both(g):
        ahead.prepare(g)
        ahead.apply(g)

    def emit_resid(cols, value):
        resid[:, cols] = value.astype(BF16)

    ahead.run(both, first.forward, (8, 6, 5, 3, 0, 0, 0, 0), emit_resid)
    resid_put = pltpu.make_async_copy(resid, resid_hbm, put_sem.at[8])
    resid_put.start()
    scale = row_scale(resid)

    puts = [
        gather_half(
            h, pick, packed, send2, put_sem.at[2 + h],
            lambda cols: (resid[:, cols].astype(F32) * scale).astype(BF16),
        )
        for h in range(2)
    ]
    puts[0].wait()
    second.start_far(0)
    puts[1].wait()
    second.start_far(1)
    second.start_near(ORDER[:9])

    first.wait_near(ORDER[:9])
    first.wait_far()
    load(7, got1, got).wait()
    wd_load.wait()

    def back_tile(n, _):
        part = columns(n, HTILE)
        back[:, part] = nt(got[...], wd[part, :])
        return 0

    lax.fori_loop(0, HID // HTILE, back_tile, 0)
    wu_load.wait()
    second.forward()
    for g in range(2):
        group = pl.ds(g * GROUP, GROUP)
        if g == 0:
            second.wait_near(ORDER[:8])
        else:
            second.wait_near(ORDER[8:9])
            second.wait_far()
        load(8 + g, got2.at[group], rows.at[g]).wait()

        def up_tile(n, _):
            part = columns(n, HTILE)
            pre = nn(rows[g], wu[:, part])
            sig = 1.0 / (1.0 + jnp.exp(-pre))
            act[group, part] = (pre * sig).astype(BF16)
            pre_grad[group, part] = (
                back[group, part] * sig * (1.0 + pre * (1.0 - sig))
            ).astype(BF16)
            return 0

        lax.fori_loop(0, HID // HTILE, up_tile, 0)

        def grad_tile(n, _):
            part = columns(n, FTILE)
            packed[group, part] = nt(pre_grad[group, :], wu[part, :]).astype(BF16)
            return 0

        lax.fori_loop(0, D // FTILE, grad_tile, 0)
        put = pltpu.make_async_copy(packed.at[group], send3.at[group], put_sem.at[4 + g])
        put.start()
        put.wait()
        if g == 0:
            third.start_near(ORDER[:8])
        else:
            third.start_far(0)
            third.start_far(1)
            third.start_near(ORDER[8:9])

    def out_tile(n, _):
        part = columns(n, FTILE)
        packed[:, part] = nn(act[...], wd[:, part]).astype(BF16)
        return 0

    lax.fori_loop(0, D // FTILE, out_tile, 0)
    out_put = pltpu.make_async_copy(packed, send4, put_sem.at[6])
    out_put.start()
    high, low = weight_matrices(slots, gate_ref)
    high_ref[...] = high
    low_ref[...] = low
    weight_puts = [
        pltpu.make_async_copy(s, d, put_sem.at[9 + k])
        for k, (s, d) in enumerate([(high_ref, high_hbm), (low_ref, low_hbm)])
    ]
    for put in weight_puts:
        put.start()
    third.forward()
    out_put.wait()

    fourth.start_far(0)
    fourth.start_far(1)
    fourth.start_near(ORDER[:9])
    behind = Pass(
        False, here, facts, ld_ref, b, c, dres, refs, bwd_in, out_buf.at[1], chain_sem.at[1]
    )

    def prepare(g, _):
        behind.prepare(g)
        return 0

    lax.fori_loop(0, H // 8, prepare, 0)
    third.wait_near(ORDER[:9])
    third.wait_far()
    load(10, got3, got).wait()

    def combine(n, total):
        cols = columns(n, CW)
        dmixed = nn(high, got[:, cols]) + nn(low, got[:, cols])
        inner[:, cols] = dmixed
        return total + dmixed * (resid[:, cols].astype(F32) * scale)

    total = lax.fori_loop(0, D // CW, combine, jnp.zeros((T, CW), F32))
    mean = jnp.sum(total, axis=1, keepdims=True) / D

    def finish_rows(n, _):
        cols = columns(n, CW)
        normed = resid[:, cols].astype(F32) * scale
        dres[:, cols] = (
            cot_ref[:, cols].astype(F32) + scale * (inner[:, cols] - normed * mean)
        ).astype(BF16)
        return 0

    lax.fori_loop(0, D // CW, finish_rows, 0)

    def emit_dx(cols, value):
        dx_ref[:, cols] = value.astype(BF16)

    behind.run(behind.apply, fourth.forward, (0,) * NSEQ, emit_dx)
    dx_put = pltpu.make_async_copy(dx_ref, dx_hbm, put_sem.at[7])
    dx_put.start()
    fourth.wait_near(ORDER[:9])
    fourth.wait_far()
    dx_put.wait()
    resid_put.wait()
    for put in weight_puts:
        put.wait()
    for exchange in (first, second, third, fourth):
        exchange.finish()


def output_kernel(high_ref, low_ref, got_ref, resid_ref, dx_ref, output_ref, grad_ref):
    def step(n, _):
        cols = columns(n, CW)
        moe = nn(high_ref[...], got_ref[:, cols]) + nn(low_ref[...], got_ref[:, cols])
        output_ref[:, cols] = (resid_ref[:, cols].astype(F32) + moe).astype(BF16)
        grad_ref[:, cols] = dx_ref[:, cols]
        return 0

    lax.fori_loop(0, D // CW, step, 0)


VM = pl.BlockSpec(memory_space=pltpu.VMEM)
SM = pl.BlockSpec(memory_space=pltpu.SMEM)
HB = pl.BlockSpec(memory_space=pltpu.HBM)
ROWS = jax.ShapeDtypeStruct((SLOTS, D), BF16)
STAGE = jax.ShapeDtypeStruct((len(FAR), 2, CAP, HALF), BF16)
TOKENS = jax.ShapeDtypeStruct((T, D), BF16)
WEIGHTS = jax.ShapeDtypeStruct((T, SLOTS), BF16)


def on_device(
    inputs, b_proj, c_proj, log_decay, doc_lengths, expert_ids, gate_weights, w_up, w_down,
    cotangent,
):
    outs = [TOKENS, TOKENS, WEIGHTS, WEIGHTS, ROWS]
    outs += [ROWS, ROWS, STAGE] * 3 + [ROWS, STAGE]
    resid, dx, high, low, got = pl.pallas_call(
        layer_kernel,
        out_shape=outs,
        in_specs=[SM] + [HB] * 4 + [VM] * 2 + [HB] * 3,
        out_specs=[HB] * len(outs),
        scratch_shapes=[
            pltpu.VMEM((T, D), BF16),
            pltpu.VMEM((T, D), BF16),
            pltpu.VMEM((T, T), BF16),
            pltpu.VMEM((T, T), BF16),
            pltpu.VMEM((H, T), F32),
            pltpu.VMEM((T, D), BF16),
            pltpu.VMEM((T, D), BF16),
            pltpu.VMEM((T, D), BF16),
            pltpu.VMEM((T, SLOTS), BF16),
            pltpu.VMEM((T, SLOTS), BF16),
            pltpu.VMEM((SLOTS, D), BF16),
            pltpu.VMEM((SLOTS, D), BF16),
            pltpu.VMEM((2, GROUP, D), BF16),
            pltpu.VMEM((D, HID), BF16),
            pltpu.VMEM((HID, D), BF16),
            pltpu.VMEM((SLOTS, HID), F32),
            pltpu.VMEM((SLOTS, HID), BF16),
            pltpu.VMEM((SLOTS, HID), BF16),
            pltpu.VMEM((H, 2 * T, T), BF16),
            pltpu.VMEM((T, D), F32),
            pltpu.VMEM((CHUNKS, T, CW), F32),
            pltpu.VMEM((H // 8, T, 8), F32),
            pltpu.VMEM((CHUNKS, 8, CW), F32),
            pltpu.VMEM((CHUNKS, T, CW), BF16),
            pltpu.VMEM((CHUNKS, T, CW), BF16),
            pltpu.VMEM((2, CHUNKS, T, CW), BF16),
            pltpu.SemaphoreType.DMA((2, 2, CHUNKS)),
            pltpu.SemaphoreType.DMA((11,)),
            pltpu.SemaphoreType.DMA((11,)),
        ]
        + EXCHANGE_SEMS * 4,
        compiler_params=pltpu.CompilerParams(
            collective_id=1, has_side_effects=True, vmem_limit_bytes=VMEM_LIMIT
        ),
    )(
        doc_lengths, inputs[0], b_proj[0], c_proj[0], log_decay[0], expert_ids[0].T,
        gate_weights[0].T, w_up[0], w_down[0], cotangent[0],
    )[:5]
    output, grad = pl.pallas_call(
        output_kernel,
        out_shape=[TOKENS, TOKENS],
        in_specs=[VM] * 5,
        out_specs=[VM, VM],
        compiler_params=pltpu.CompilerParams(vmem_limit_bytes=VMEM_LIMIT),
    )(high, low, got, resid, dx)
    return (output[None], grad[None])


def solution(mesh):
    rows = P("exp", "seq", None)
    whole = P("exp", None, None)
    return jax.shard_map(
        on_device,
        mesh=mesh,
        in_specs=(
            rows, rows, rows, P("exp", None, "seq"), P("exp", None), rows, rows, whole, whole,
            rows,
        ),
        out_specs=(rows, rows),
        check_vma=False,
    )
```
